32 devices in a mesh: wide: 8 (over z, x), chol: 4 (over y, core).
Axes of the slice: x: 2, y: 2, z: 4, core: 2. Of those that a mesh axis runs over, the one named last changes fastest.
Arguments:
- walkers: bfloat16 [8, 2048, 256], P('wide', 'chol'), may hold values from -6 to 6
- intersection_inv: bfloat16 [8, 256, 256], P('wide'), may hold values from -0.375 to 0.375
- trial_state: bfloat16 [2048, 256], replicated, may hold values from -0.125 to 0.125
- chol_tiles: bfloat16 [2048, 128, 128], P(('wide', 'chol')), may hold values from -1.25 to 1.25
- tile_vector: int32 [2048], P(('wide', 'chol')), may hold values from 0 to 63
- tile_row: int32 [2048], P(('wide', 'chol')), may hold values from 0 to 15
- tile_col: int32 [2048], P(('wide', 'chol')), may hold values from 0 to 3
- tile_count: int32 [32], P(('wide', 'chol')), may hold values from 32 to 64, as said below
- sources: int32 [8], replicated, may hold values from 0 to 7
- aux_noise: float32 [8, 512], P(None, 'wide'), may hold values from -6 to 6
Outputs:
- force_bias: float32 [8, 512], P(None, 'wide')
- new_walkers: bfloat16 [8, 2048, 256], P('wide', 'chol')
The draws below stay inside these ranges and needn't reach their ends.
Inputs may be any that keep to these rules, and one draw needn't show every extreme that they name: `tile_count`: slots beyond a device's count are ignored; some device has all 64 slots live.
All inputs are finite; a program needn't handle non-finite values.
Results may differ from the reference program's by a relative error of at most 0.019.
Values may be sent and summed in bfloat16 or wider, within the bound.
A program may use at most 192 MiB of HBM per device.

```python
import jax
import jax.numpy as jnp
from jax import lax

ORB = 2048
NEL = 256
TB = 128
TAYLOR = 4
VEC_DEV = 64
TILE_CAP = 64
WALKERS = 8
VEC = 512
ORB_DEV = 512
NTILE = 16
COLBLK = 4
N_CHOL = 4
DEVICES = 32


def draw_tile_count(key, part):
    first, second = jax.random.split(key)
    counts = jax.random.randint(first, (DEVICES,), TILE_CAP // 2, TILE_CAP + 1)
    where = jax.random.randint(second, (), 0, DEVICES)
    return jnp.where(jnp.arange(DEVICES) == where, TILE_CAP, counts).astype(jnp.int32)


def plant(drawn, own_key, smallest, high):
    longest = drawn.shape.index(max(drawn.shape))
    spots = []
    for shift in (0, 1):
        where = [jax.random.randint(jax.random.fold_in(own_key, axis), (), 0, length) for axis, length in enumerate(drawn.shape)]
        where[longest] = (where[longest] + shift) % drawn.shape[longest]
        spots.append(tuple(where))
    return drawn.at[spots[0]].set(smallest).at[spots[1]].set(high)


def steps_of(own_key, extent, cuts, low, largest):
    factor_of = 1.0
    for position, blocks in cuts:
        steps = jax.random.uniform(jax.random.fold_in(jax.random.fold_in(own_key, 6), position), (blocks,), jnp.float32, low / len(cuts), largest / len(cuts))
        factor_of = factor_of * jnp.repeat(jnp.exp(steps), extent[position] // blocks).reshape((-1,) + (1,) * (len(extent) - 1 - position))
    return factor_of


def normal_values(key, dims, scale, most, shards=(), kind=jnp.bfloat16):
    gain = steps_of(key, dims, shards, -0.22, 0.18) if shards else 1.0
    array = jax.random.normal(key, dims, jnp.float32) * scale * gain
    return jnp.minimum(jnp.maximum(array, -most), most).astype(kind)


def setup_inputs(seed: int = 0) -> dict:
    arg_keys = jax.random.split(jax.random.key(seed), 11)
    return {
        "walkers": normal_values(arg_keys[0], (WALKERS, ORB, NEL), 1.0, 6.0, ((0, 8), (1, 4))),
        "intersection_inv": normal_values(arg_keys[1], (WALKERS, NEL, NEL), NEL ** -0.5, 0.375, ((0, 8),)),
        "trial_state": normal_values(arg_keys[2], (ORB, NEL), ORB ** -0.5, 0.125),
        "chol_tiles": normal_values(arg_keys[3], (TILE_CAP * DEVICES, TB, TB), (10 * ORB * TB ** -1 * (ORB * TILE_CAP * DEVICES) ** -0.5), 1.25, ((0, 32),)),
        "tile_vector": plant(jax.random.randint(arg_keys[4], (TILE_CAP * DEVICES,), 0, VEC_DEV), jax.random.fold_in(arg_keys[4], 1), 0, VEC_DEV - 1).astype(jnp.int32),
        "tile_row": plant(jax.random.randint(arg_keys[5], (TILE_CAP * DEVICES,), 0, NTILE), jax.random.fold_in(arg_keys[5], 1), 0, NTILE - 1).astype(jnp.int32),
        "tile_col": plant(jax.random.randint(arg_keys[6], (TILE_CAP * DEVICES,), 0, COLBLK), jax.random.fold_in(arg_keys[6], 1), 0, COLBLK - 1).astype(jnp.int32),
        "tile_count": draw_tile_count(jax.random.fold_in(arg_keys[10], 71), 0),
        "sources": plant(jax.random.randint(arg_keys[8], (WALKERS,), 0, WALKERS), jax.random.fold_in(arg_keys[8], 1), 0, WALKERS - 1).astype(jnp.int32),
        "aux_noise": normal_values(arg_keys[9], (WALKERS, VEC), 1.0, 6.0, ((1, 8),), jnp.float32),
    }


SQRT_TAU = 0.1


def reference(walkers, intersection_inv, trial_state, chol_tiles, tile_vector, tile_row, tile_col, tile_count, sources, aux_noise):
    f32 = jnp.float32
    bf16 = jnp.bfloat16
    theta = jnp.einsum('wmn,wnk->wmk', walkers.astype(f32), intersection_inv.astype(f32)).astype(bf16)
    theta_new = jnp.take(theta, sources, axis=0)
    picked = jnp.take(walkers, sources, axis=0)
    trial_blocks = trial_state.reshape(NTILE, TB, NEL)
    slots = jnp.arange(TILE_CAP * DEVICES, dtype=jnp.int32)
    device = slots // TILE_CAP
    live = ((slots % TILE_CAP) < jnp.take(tile_count, device)).astype(f32)
    columns = (device % N_CHOL) * COLBLK + tile_col
    vectors = (device // N_CHOL) * VEC_DEV + tile_vector
    zero = jnp.zeros((), jnp.int32)

    def bias_step(total, item):
        tile, row, column, vector, weight = item
        rows_here = lax.dynamic_index_in_dim(trial_blocks, row, 0, keepdims=False)
        projected = jnp.dot(tile.T, rows_here, preferred_element_type=f32).astype(bf16)
        projected = lax.optimization_barrier(projected).astype(f32)
        block = lax.dynamic_slice(theta_new, (zero, column * TB, zero), (WALKERS, TB, NEL)).astype(f32)
        value = jnp.sum(block * projected[None], axis=(1, 2)) * weight
        return total.at[:, vector].add(value), None

    force_bias, _ = lax.scan(bias_step, jnp.zeros((WALKERS, VEC), f32),
                             (chol_tiles, tile_row, columns, vectors, live))
    field = (aux_noise - SQRT_TAU * force_bias).astype(bf16)
    field_wide = field.astype(f32)

    def device_step(operator, item):
        tiles_here, rows_here, cols_here, vecs_here, live_here, chol_index = item

        def tile_step(part, inner):
            tile, row, column, vector, weight = inner
            coef = lax.dynamic_index_in_dim(field_wide, vector, 1, keepdims=False) * weight
            start = (zero, row * TB, column * TB)
            block = lax.dynamic_slice(part, start, (WALKERS, TB, TB)) + coef[:, None, None] * tile.astype(f32)[None]
            return lax.dynamic_update_slice(part, block, start), None

        part, _ = lax.scan(tile_step, jnp.zeros((WALKERS, ORB, ORB_DEV), f32),
                           (tiles_here, rows_here, cols_here, vecs_here, live_here))
        rounded = lax.optimization_barrier(part.astype(bf16)).astype(f32)
        start = (zero, zero, chol_index * ORB_DEV)
        merged = lax.dynamic_slice(operator, start, (WALKERS, ORB, ORB_DEV)) + rounded
        return lax.dynamic_update_slice(operator, merged, start), None

    items = (chol_tiles.reshape(DEVICES, TILE_CAP, TB, TB), tile_row.reshape(DEVICES, TILE_CAP),
             tile_col.reshape(DEVICES, TILE_CAP), vectors.reshape(DEVICES, TILE_CAP),
             live.reshape(DEVICES, TILE_CAP), jnp.arange(DEVICES, dtype=jnp.int32) % N_CHOL)
    operator, _ = lax.scan(device_step, jnp.zeros((WALKERS, ORB, ORB), f32), items)
    operator = lax.optimization_barrier(operator.astype(bf16)).astype(f32)
    term = picked
    total = picked.astype(f32)
    for order in range(1, TAYLOR + 1):
        product = jnp.einsum('wpq,wqn->wpn', operator, term.astype(f32))
        term = (SQRT_TAU / order * product).astype(bf16)
        total = total + term.astype(f32)
    return force_bias, total.astype(bf16)
```

```python
import jax
import jax.numpy as jnp
from jax import lax
from jax.sharding import PartitionSpec as P

TAYLOR = 4


SQRT_TAU = 0.1


def ring_order(size):
    half = size // 2
    return [2 * p for p in range(half)] + [2 * (size - 1 - p) + 1 for p in range(half, size)]


def body(
    walkers,
    intersection_inv,
    trial_state,
    chol_tiles,
    tile_vector,
    tile_row,
    tile_col,
    tile_count,
    sources,
    aux_noise,
):
    f32 = jnp.float32
    bf16 = jnp.bfloat16
    highest = lax.Precision.HIGHEST
    walk_dev, orb_rows, electrons = walkers.shape
    slot_count, tile_size, _ = chol_tiles.shape
    orbitals = trial_state.shape[0]
    row_blocks = orbitals // tile_size
    col_blocks = orb_rows // tile_size
    walk_all, vec_dev = aux_noise.shape
    wide = lax.axis_size("wide")
    me = lax.axis_index("wide")
    live_slot = jnp.arange(slot_count, dtype=jnp.int32) < tile_count[0]
    place_own = jnp.where(live_slot, tile_row * col_blocks + tile_col, -1)
    meta = lax.all_gather(jnp.stack([place_own, tile_vector]), "wide", axis=0)
    walker_rows = lax.all_gather(walkers, "wide", axis=0, tiled=True)
    inv_all = lax.all_gather(intersection_inv, "wide", axis=0, tiled=True)
    order = ring_order(wide)
    right = [(order[p], order[(p + 1) % wide]) for p in range(wide)]
    left = [(b, a) for a, b in right]
    spot_of = [0] * wide
    for p, idx in enumerate(order):
        spot_of[idx] = p
    turns = [0] + [turn for step in range(1, wide) for turn in (-step, step)]
    owners = jnp.asarray(
        [[order[(spot_of[idx] + turn) % wide] for turn in turns] for idx in range(wide)], jnp.int32
    )[me]
    half = slot_count // 2
    going, coming = chol_tiles[:half], chol_tiles[half:]
    parts = [chol_tiles]
    for step in range(1, wide):
        going = lax.ppermute(going, "wide", right)
        coming = lax.ppermute(coming, "wide", left)
        parts += [going, coming]
    picker = (sources[:, None] == jnp.arange(walk_all, dtype=jnp.int32)[None, :]).astype(bf16)
    picked = jnp.einsum("jw,wmn->jmn", picker, walker_rows, preferred_element_type=f32).astype(bf16)
    picked_inv = jnp.einsum("jw,wnk->jnk", picker, inv_all, preferred_element_type=f32).astype(bf16)
    theta_new = jnp.einsum("jmn,jnk->jmk", picked, picked_inv, preferred_element_type=f32).astype(
        bf16
    )
    own_walkers = lax.dynamic_slice_in_dim(picked, me * walk_dev, walk_dev, 0)
    row_hot = (tile_row[:, None] == jnp.arange(row_blocks, dtype=jnp.int32)[None, :]).astype(f32)
    col_hot = (tile_col[:, None] == jnp.arange(col_blocks, dtype=jnp.int32)[None, :]).astype(f32)
    live = live_slot.astype(f32)
    vec_hot = (tile_vector[:, None] == jnp.arange(vec_dev, dtype=jnp.int32)[None, :]).astype(f32)
    trial_blocks = trial_state.reshape(row_blocks, tile_size * electrons)
    tile_rows = jnp.dot(row_hot.astype(bf16), trial_blocks, preferred_element_type=f32).astype(bf16)
    tile_rows = tile_rows.reshape(slot_count, tile_size, electrons)
    projected = jnp.einsum(
        "tpq,tpn->tqn", chol_tiles, tile_rows, preferred_element_type=f32
    ).astype(bf16)
    theta_blocks = theta_new.reshape(walk_all, col_blocks, tile_size, electrons)
    scores = jnp.einsum("tqn,wcqn->wtc", projected, theta_blocks, preferred_element_type=f32)
    scores = jnp.sum(scores * col_hot[None], axis=2) * live[None, :]
    bias_part = jnp.dot(scores, vec_hot, precision=highest)
    force_bias = lax.psum(bias_part, "chol")
    field = (aux_noise - SQRT_TAU * force_bias).astype(bf16)
    field_all = lax.all_gather(field, "wide", axis=0)
    own_field = lax.dynamic_index_in_dim(field_all, me * walk_dev, 1, keepdims=False)
    places = row_blocks * col_blocks
    place_all, vec_all = meta[:, 0], meta[:, 1]
    vec_hot_all = (vec_all[:, :, None] == jnp.arange(vec_dev, dtype=jnp.int32)).astype(f32)
    coeff = jnp.sum(vec_hot_all * own_field.astype(f32)[:, None, :], axis=2)

    def in_parts(whole):
        picked_rows = jnp.sum(
            jnp.where(
                owners[:, None, None] == jnp.arange(wide, dtype=jnp.int32)[None, :, None],
                whole[None],
                jnp.zeros((), whole.dtype),
            ),
            axis=1,
        )
        ends = jnp.stack([picked_rows[1::2, :half], picked_rows[2::2, half:]], axis=1)
        return jnp.concatenate([picked_rows[0], ends.reshape(-1)])

    weights_in = jnp.where(
        in_parts(place_all)[None, :] == jnp.arange(places, dtype=jnp.int32)[:, None],
        in_parts(coeff)[None, :],
        0.0,
    ).astype(bf16)
    tiles_in = jnp.concatenate(parts, axis=0)
    spread = jnp.einsum(
        "akt,tpq->apkq",
        weights_in.reshape(row_blocks, col_blocks, -1),
        tiles_in,
        preferred_element_type=f32,
    ).astype(bf16)
    own_op = spread.reshape(1, orbitals, orb_rows)
    term = own_walkers
    total = own_walkers.astype(f32)
    for order in range(1, TAYLOR + 1):
        product = jnp.einsum("wpm,wmn->pwn", own_op, term, preferred_element_type=f32)
        summed = lax.psum_scatter(
            product.astype(bf16), "chol", scatter_dimension=0, tiled=True
        ).astype(f32)
        term = (SQRT_TAU / order * jnp.transpose(summed, (1, 0, 2))).astype(bf16)
        total = total + term.astype(f32)
    return (force_bias, total.astype(bf16))


def solution(mesh):
    return jax.shard_map(
        body,
        mesh=mesh,
        in_specs=(
            P("wide", "chol", None),
            P("wide", None, None),
            P(),
            P(("wide", "chol"), None, None),
            P(("wide", "chol")),
            P(("wide", "chol")),
            P(("wide", "chol")),
            P(("wide", "chol")),
            P(),
            P(None, "wide"),
        ),
        out_specs=(P(None, "wide"), P("wide", "chol", None)),
        check_vma=False,
    )
```

```python
import functools

import jax
import jax.numpy as jnp
from jax import lax
from jax.experimental import pallas as pl
from jax.experimental.pallas import tpu as pltpu
from jax.sharding import PartitionSpec as P

TAYLOR = 4


SQRT_TAU = 0.1


def ring_order(size):
    half = size // 2
    return [2 * p for p in range(half)] + [2 * (size - 1 - p) + 1 for p in range(half, size)]


def series_kernel(
    pairs,
    op_ref,
    walk_ref,
    out_ref,
    op_peer,
    walk_in,
    term,
    total,
    send_buf,
    recv_buf,
    end_send,
    end_recv,
    swap_send,
    swap_recv,
    send_sem,
    recv_sem,
):
    f32 = jnp.float32
    bf16 = jnp.bfloat16
    wide = lax.axis_index("wide")
    me = lax.axis_index("chol")
    core = me % 2
    pair = me // 2
    partner = me + 1 - 2 * core
    rows = op_ref.shape[1]
    chunks = send_buf.shape[2]
    piece = send_buf.shape[3]
    peers = [((pair + j) % pairs) for j in range(1, pairs)]

    def place(chol):
        return (wide, chol)

    barrier = pltpu.get_barrier_semaphore()
    for other in [partner] + [2 * p + core for p in peers]:
        pl.semaphore_signal(
            barrier, inc=1, device_id=place(other), device_id_type=pl.DeviceIdType.MESH
        )
    pl.semaphore_wait(barrier, pairs)

    def remote(src, dst, send, recv, other):
        return pltpu.make_async_remote_copy(
            src_ref=src,
            dst_ref=dst,
            send_sem=send,
            recv_sem=recv,
            device_id=place(other),
            device_id_type=pl.DeviceIdType.MESH,
        )

    walk_swap = remote(
        walk_ref.at[1 - core], walk_in, swap_send.at[0], swap_recv.at[0], partner
    )
    op_swap = remote(op_ref, op_peer, swap_send.at[1], swap_recv.at[1], partner)
    walk_swap.start()
    op_swap.start()
    own_at = pl.ds(pl.multiple_of(core * rows, rows), rows)
    other_at = pl.ds(pl.multiple_of((1 - core) * rows, rows), rows)
    term[own_at, :] = walk_ref[core]
    total[own_at, :] = walk_ref[core].astype(f32)
    walk_swap.wait()
    term[other_at, :] = walk_in[...]
    total[other_at, :] = walk_in[...].astype(f32)
    op_swap.wait()

    def product(start, count):
        at = pl.ds(pl.multiple_of(start, piece), count)
        return jnp.dot(op_ref[at, :], term[own_at, :], preferred_element_type=f32) + jnp.dot(
            op_peer[at, :], term[other_at, :], preferred_element_type=f32
        )

    for order in range(1, TAYLOR + 1):
        copies = []
        for j, p in enumerate(peers):
            for c in range(chunks):
                slot = (order - 1, j, c)
                send_buf[slot] = product(p * (2 * rows) + c * piece, piece).astype(bf16)
                copy = remote(
                    send_buf.at[slot],
                    recv_buf.at[slot],
                    send_sem.at[slot],
                    recv_sem.at[slot],
                    2 * p + core,
                )
                copy.start()
                copies.append(copy)
        parts = [product(pair * (2 * rows) + c * piece, piece) for c in range(chunks)]
        for c in range(chunks):
            part = parts[c]
            for j in range(len(peers)):
                copies[j * chunks + c].wait()
                part = part + recv_buf[order - 1, j, c].astype(f32)
            parts[c] = (SQRT_TAU / order * part).astype(bf16)
        for c in range(chunks):
            at = pl.ds(c * piece, piece)
            term[at, :] = parts[c]
            total[at, :] += parts[c].astype(f32)
    end_send[...] = total[other_at, :].astype(bf16)
    end_swap = remote(end_send, end_recv, swap_send.at[2], swap_recv.at[2], partner)
    end_swap.start()
    out_ref[core] = total[own_at, :].astype(bf16)
    end_swap.wait()
    out_ref[1 - core] = end_recv[...]


def taylor(own_op, own_walkers, chol):
    bf16 = jnp.bfloat16
    orbitals, rows = own_op.shape
    electrons = own_walkers.shape[1]
    half = electrons // 2
    pairs = chol // 2
    chunks = 4
    piece = 2 * rows // chunks
    others = max(pairs - 1, 1)
    slots = (TAYLOR, others, chunks)
    walk = jnp.transpose(own_walkers.reshape(rows, 2, half), (1, 0, 2))
    out = pl.pallas_call(
        functools.partial(series_kernel, pairs),
        out_shape=jax.ShapeDtypeStruct((2, rows, half), bf16),
        in_specs=[pl.BlockSpec(memory_space=pltpu.VMEM)] * 2,
        out_specs=pl.BlockSpec(memory_space=pltpu.VMEM),
        scratch_shapes=[
            pltpu.VMEM((orbitals, rows), bf16),
            pltpu.VMEM((rows, half), bf16),
            pltpu.VMEM((2 * rows, half), bf16),
            pltpu.VMEM((2 * rows, half), jnp.float32),
            pltpu.VMEM(slots + (piece, half), bf16),
            pltpu.VMEM(slots + (piece, half), bf16),
            pltpu.VMEM((rows, half), bf16),
            pltpu.VMEM((rows, half), bf16),
            pltpu.SemaphoreType.DMA((3,)),
            pltpu.SemaphoreType.DMA((3,)),
            pltpu.SemaphoreType.DMA(slots),
            pltpu.SemaphoreType.DMA(slots),
        ],
        compiler_params=pltpu.CompilerParams(
            collective_id=0, has_side_effects=True, vmem_limit_bytes=32 * 1024 * 1024
        ),
    )(own_op, walk)
    return jnp.transpose(out, (1, 0, 2)).reshape(rows, electrons)


def body(
    walkers,
    intersection_inv,
    trial_state,
    chol_tiles,
    tile_vector,
    tile_row,
    tile_col,
    tile_count,
    sources,
    aux_noise,
):
    f32 = jnp.float32
    bf16 = jnp.bfloat16
    highest = lax.Precision.HIGHEST
    walk_dev, orb_rows, electrons = walkers.shape
    slot_count, tile_size, _ = chol_tiles.shape
    orbitals = trial_state.shape[0]
    row_blocks = orbitals // tile_size
    col_blocks = orb_rows // tile_size
    walk_all, vec_dev = aux_noise.shape
    wide = lax.axis_size("wide")
    me = lax.axis_index("wide")
    live_slot = jnp.arange(slot_count, dtype=jnp.int32) < tile_count[0]
    place_own = jnp.where(live_slot, tile_row * col_blocks + tile_col, -1)
    meta = lax.all_gather(jnp.stack([place_own, tile_vector]), "wide", axis=0)
    walker_rows = lax.all_gather(walkers, "wide", axis=0, tiled=True)
    inv_all = lax.all_gather(intersection_inv, "wide", axis=0, tiled=True)
    order = ring_order(wide)
    right = [(order[p], order[(p + 1) % wide]) for p in range(wide)]
    left = [(b, a) for a, b in right]
    spot_of = [0] * wide
    for p, idx in enumerate(order):
        spot_of[idx] = p
    turns = [0] + [turn for step in range(1, wide) for turn in (-step, step)]
    owners = jnp.asarray(
        [[order[(spot_of[idx] + turn) % wide] for turn in turns] for idx in range(wide)], jnp.int32
    )[me]
    half = slot_count // 2
    going, coming = chol_tiles[:half], chol_tiles[half:]
    parts = [chol_tiles]
    for step in range(1, wide):
        going = lax.ppermute(going, "wide", right)
        coming = lax.ppermute(coming, "wide", left)
        parts += [going, coming]
    picker = (sources[:, None] == jnp.arange(walk_all, dtype=jnp.int32)[None, :]).astype(bf16)
    picked = jnp.einsum("jw,wmn->jmn", picker, walker_rows, preferred_element_type=f32).astype(bf16)
    picked_inv = jnp.einsum("jw,wnk->jnk", picker, inv_all, preferred_element_type=f32).astype(bf16)
    theta_new = jnp.einsum("jmn,jnk->jmk", picked, picked_inv, preferred_element_type=f32).astype(
        bf16
    )
    own_walkers = lax.dynamic_slice_in_dim(picked, me * walk_dev, walk_dev, 0)
    row_hot = (tile_row[:, None] == jnp.arange(row_blocks, dtype=jnp.int32)[None, :]).astype(f32)
    col_hot = (tile_col[:, None] == jnp.arange(col_blocks, dtype=jnp.int32)[None, :]).astype(f32)
    live = live_slot.astype(f32)
    vec_hot = (tile_vector[:, None] == jnp.arange(vec_dev, dtype=jnp.int32)[None, :]).astype(f32)
    trial_blocks = trial_state.reshape(row_blocks, tile_size * electrons)
    tile_rows = jnp.dot(row_hot.astype(bf16), trial_blocks, preferred_element_type=f32).astype(bf16)
    tile_rows = tile_rows.reshape(slot_count, tile_size, electrons)
    projected = jnp.einsum(
        "tpq,tpn->tqn", chol_tiles, tile_rows, preferred_element_type=f32
    ).astype(bf16)
    theta_blocks = theta_new.reshape(walk_all, col_blocks, tile_size, electrons)
    scores = jnp.einsum("tqn,wcqn->wtc", projected, theta_blocks, preferred_element_type=f32)
    scores = jnp.sum(scores * col_hot[None], axis=2) * live[None, :]
    bias_part = jnp.dot(scores, vec_hot, precision=highest)
    force_bias = lax.psum(bias_part, "chol")
    field = (aux_noise - SQRT_TAU * force_bias).astype(bf16)
    field_all = lax.all_gather(field, "wide", axis=0)
    own_field = lax.dynamic_index_in_dim(field_all, me * walk_dev, 1, keepdims=False)
    places = row_blocks * col_blocks
    place_all, vec_all = meta[:, 0], meta[:, 1]
    vec_hot_all = (vec_all[:, :, None] == jnp.arange(vec_dev, dtype=jnp.int32)).astype(f32)
    coeff = jnp.sum(vec_hot_all * own_field.astype(f32)[:, None, :], axis=2)

    def in_parts(whole):
        picked_rows = jnp.sum(
            jnp.where(
                owners[:, None, None] == jnp.arange(wide, dtype=jnp.int32)[None, :, None],
                whole[None],
                jnp.zeros((), whole.dtype),
            ),
            axis=1,
        )
        ends = jnp.stack([picked_rows[1::2, :half], picked_rows[2::2, half:]], axis=1)
        return jnp.concatenate([picked_rows[0], ends.reshape(-1)])

    weights_in = jnp.where(
        in_parts(place_all)[None, :] == jnp.arange(places, dtype=jnp.int32)[:, None],
        in_parts(coeff)[None, :],
        0.0,
    ).astype(bf16)
    tiles_in = jnp.concatenate(parts, axis=0)
    spread = jnp.einsum(
        "akt,tpq->apkq",
        weights_in.reshape(row_blocks, col_blocks, -1),
        tiles_in,
        preferred_element_type=f32,
    ).astype(bf16)
    own_op = spread.reshape(1, orbitals, orb_rows)
    total = taylor(own_op[0], own_walkers[0], lax.axis_size("chol"))
    return (force_bias, total[None])


def solution(mesh):
    return jax.shard_map(
        body,
        mesh=mesh,
        in_specs=(
            P("wide", "chol", None),
            P("wide", None, None),
            P(),
            P(("wide", "chol"), None, None),
            P(("wide", "chol")),
            P(("wide", "chol")),
            P(("wide", "chol")),
            P(("wide", "chol")),
            P(),
            P(None, "wide"),
        ),
        out_specs=(P(None, "wide"), P("wide", "chol", None)),
        check_vma=False,
    )
```

```python
import functools

import jax
import jax.numpy as jnp
from jax import lax
from jax.experimental import pallas as pl
from jax.experimental.pallas import tpu as pltpu
from jax.sharding import PartitionSpec as P

TAYLOR = 4


SQRT_TAU = 0.1


def ring_order(size):
    half = size // 2
    return [2 * p for p in range(half)] + [2 * (size - 1 - p) + 1 for p in range(half, size)]


def series_kernel(
    pairs,
    op_ref,
    walk_ref,
    out_ref,
    op_peer,
    walk_in,
    term,
    total,
    send_buf,
    recv_buf,
    end_send,
    end_recv,
    swap_send,
    swap_recv,
    send_sem,
    recv_sem,
):
    f32 = jnp.float32
    bf16 = jnp.bfloat16
    wide = lax.axis_index("wide")
    me = lax.axis_index("chol")
    core = me % 2
    pair = me // 2
    partner = me + 1 - 2 * core
    rows = op_ref.shape[1]
    chunks = send_buf.shape[2]
    piece = send_buf.shape[3]
    peers = [((pair + j) % pairs) for j in range(1, pairs)]

    def place(chol):
        return (wide, chol)

    barrier = pltpu.get_barrier_semaphore()
    for other in [partner] + [2 * p + core for p in peers]:
        pl.semaphore_signal(
            barrier, inc=1, device_id=place(other), device_id_type=pl.DeviceIdType.MESH
        )
    pl.semaphore_wait(barrier, pairs)

    def remote(src, dst, send, recv, other):
        return pltpu.make_async_remote_copy(
            src_ref=src,
            dst_ref=dst,
            send_sem=send,
            recv_sem=recv,
            device_id=place(other),
            device_id_type=pl.DeviceIdType.MESH,
        )

    walk_swap = remote(
        walk_ref.at[1 - core], walk_in, swap_send.at[0], swap_recv.at[0], partner
    )
    op_swap = remote(op_ref, op_peer, swap_send.at[1], swap_recv.at[1], partner)
    walk_swap.start()
    op_swap.start()
    own_at = pl.ds(pl.multiple_of(core * rows, rows), rows)
    other_at = pl.ds(pl.multiple_of((1 - core) * rows, rows), rows)
    term[own_at, :] = walk_ref[core]
    total[own_at, :] = walk_ref[core].astype(f32)
    walk_swap.wait()
    term[other_at, :] = walk_in[...]
    total[other_at, :] = walk_in[...].astype(f32)
    op_swap.wait()

    def product(start, count):
        at = pl.ds(pl.multiple_of(start, piece), count)
        return jnp.dot(op_ref[at, :], term[own_at, :], preferred_element_type=f32) + jnp.dot(
            op_peer[at, :], term[other_at, :], preferred_element_type=f32
        )

    for order in range(1, TAYLOR + 1):
        copies = []
        for j, p in enumerate(peers):
            for c in range(chunks):
                slot = (order - 1, j, c)
                send_buf[slot] = product(p * (2 * rows) + c * piece, piece).astype(bf16)
                copy = remote(
                    send_buf.at[slot],
                    recv_buf.at[slot],
                    send_sem.at[slot],
                    recv_sem.at[slot],
                    2 * p + core,
                )
                copy.start()
                copies.append(copy)
        parts = [product(pair * (2 * rows) + c * piece, piece) for c in range(chunks)]
        for c in range(chunks):
            part = parts[c]
            for j in range(len(peers)):
                copies[j * chunks + c].wait()
                part = part + recv_buf[order - 1, j, c].astype(f32)
            parts[c] = (SQRT_TAU / order * part).astype(bf16)
        for c in range(chunks):
            at = pl.ds(c * piece, piece)
            term[at, :] = parts[c]
            total[at, :] += parts[c].astype(f32)
    end_send[...] = total[other_at, :].astype(bf16)
    end_swap = remote(end_send, end_recv, swap_send.at[2], swap_recv.at[2], partner)
    end_swap.start()
    out_ref[core] = total[own_at, :].astype(bf16)
    end_swap.wait()
    out_ref[1 - core] = end_recv[...]


def taylor(own_op, own_walkers, chol):
    bf16 = jnp.bfloat16
    orbitals, rows = own_op.shape
    electrons = own_walkers.shape[1]
    half = electrons // 2
    pairs = chol // 2
    chunks = 4
    piece = 2 * rows // chunks
    others = max(pairs - 1, 1)
    slots = (TAYLOR, others, chunks)
    walk = jnp.transpose(own_walkers.reshape(rows, 2, half), (1, 0, 2))
    out = pl.pallas_call(
        functools.partial(series_kernel, pairs),
        out_shape=jax.ShapeDtypeStruct((2, rows, half), bf16),
        in_specs=[pl.BlockSpec(memory_space=pltpu.VMEM)] * 2,
        out_specs=pl.BlockSpec(memory_space=pltpu.VMEM),
        scratch_shapes=[
            pltpu.VMEM((orbitals, rows), bf16),
            pltpu.VMEM((rows, half), bf16),
            pltpu.VMEM((2 * rows, half), bf16),
            pltpu.VMEM((2 * rows, half), jnp.float32),
            pltpu.VMEM(slots + (piece, half), bf16),
            pltpu.VMEM(slots + (piece, half), bf16),
            pltpu.VMEM((rows, half), bf16),
            pltpu.VMEM((rows, half), bf16),
            pltpu.SemaphoreType.DMA((3,)),
            pltpu.SemaphoreType.DMA((3,)),
            pltpu.SemaphoreType.DMA(slots),
            pltpu.SemaphoreType.DMA(slots),
        ],
        compiler_params=pltpu.CompilerParams(
            collective_id=0, has_side_effects=True, vmem_limit_bytes=32 * 1024 * 1024
        ),
    )(own_op, walk)
    return jnp.transpose(out, (1, 0, 2)).reshape(rows, electrons)


def body(
    walkers,
    intersection_inv,
    trial_state,
    chol_tiles,
    tile_vector,
    tile_row,
    tile_col,
    tile_count,
    sources,
    aux_noise,
):
    f32 = jnp.float32
    bf16 = jnp.bfloat16
    highest = lax.Precision.HIGHEST
    walk_dev, orb_rows, electrons = walkers.shape
    slot_count, tile_size, _ = chol_tiles.shape
    orbitals = trial_state.shape[0]
    row_blocks = orbitals // tile_size
    col_blocks = orb_rows // tile_size
    walk_all, vec_dev = aux_noise.shape
    wide = lax.axis_size("wide")
    me = lax.axis_index("wide")
    live_slot = jnp.arange(slot_count, dtype=jnp.int32) < tile_count[0]
    place_own = tile_row * col_blocks + tile_col
    walker_rows = lax.all_gather(walkers, "wide", axis=0, tiled=True)
    inv_all = lax.all_gather(intersection_inv, "wide", axis=0, tiled=True)
    order = ring_order(wide)
    right = [(order[p], order[(p + 1) % wide]) for p in range(wide)]
    left = [(b, a) for a, b in right]
    spot_of = [0] * wide
    for p, idx in enumerate(order):
        spot_of[idx] = p
    turns = [0] + [turn for step in range(1, wide) for turn in (-step, step)]
    owners = jnp.asarray(
        [[order[(spot_of[idx] + turn) % wide] for turn in turns] for idx in range(wide)], jnp.int32
    )[me]
    picker = (sources[:, None] == jnp.arange(walk_all, dtype=jnp.int32)[None, :]).astype(bf16)
    picked = jnp.einsum("jw,wmn->jmn", picker, walker_rows, preferred_element_type=f32).astype(bf16)
    picked_inv = jnp.einsum("jw,wnk->jnk", picker, inv_all, preferred_element_type=f32).astype(bf16)
    theta_new = jnp.einsum("jmn,jnk->jmk", picked, picked_inv, preferred_element_type=f32).astype(
        bf16
    )
    own_walkers = lax.dynamic_slice_in_dim(picked, me * walk_dev, walk_dev, 0)
    row_hot = (tile_row[:, None] == jnp.arange(row_blocks, dtype=jnp.int32)[None, :]).astype(f32)
    col_hot = (tile_col[:, None] == jnp.arange(col_blocks, dtype=jnp.int32)[None, :]).astype(f32)
    live = live_slot.astype(f32)
    vec_hot = (tile_vector[:, None] == jnp.arange(vec_dev, dtype=jnp.int32)[None, :]).astype(f32)
    trial_blocks = trial_state.reshape(row_blocks, tile_size * electrons)
    tile_rows = jnp.dot(row_hot.astype(bf16), trial_blocks, preferred_element_type=f32).astype(bf16)
    tile_rows = tile_rows.reshape(slot_count, tile_size, electrons)
    projected = jnp.einsum(
        "tpq,tpn->tqn", chol_tiles, tile_rows, preferred_element_type=f32
    ).astype(bf16)
    theta_blocks = theta_new.reshape(walk_all, col_blocks, tile_size, electrons)
    scores = jnp.einsum("tqn,wcqn->wtc", projected, theta_blocks, preferred_element_type=f32)
    scores = jnp.sum(scores * col_hot[None], axis=2) * live[None, :]
    bias_part = jnp.dot(scores, vec_hot, precision=highest)
    half = slot_count // 2
    going, coming = chol_tiles[:half], chol_tiles[half:]
    parts = [chol_tiles]
    for step in range(1, wide):
        if step == wide - 1:
            going, coming, bias_part = lax.optimization_barrier((going, coming, bias_part))
        going = lax.ppermute(going, "wide", right)
        coming = lax.ppermute(coming, "wide", left)
        parts += [going, coming]
    force_bias = lax.psum(bias_part, "chol")
    field = (aux_noise - SQRT_TAU * force_bias).astype(bf16)
    coeff_own = jnp.dot(field, (vec_hot * live[:, None]).T.astype(bf16), preferred_element_type=f32)
    sent = jnp.concatenate([coeff_own.astype(bf16), place_own.astype(bf16)[None]], axis=0)
    got = lax.all_gather(sent, "wide", axis=0).astype(f32)
    coeff = lax.dynamic_index_in_dim(got, me * walk_dev, 1, keepdims=False)
    place_all = got[:, walk_all].astype(jnp.int32)
    places = row_blocks * col_blocks

    def in_parts(whole):
        picked_rows = jnp.sum(
            jnp.where(
                owners[:, None, None] == jnp.arange(wide, dtype=jnp.int32)[None, :, None],
                whole[None],
                jnp.zeros((), whole.dtype),
            ),
            axis=1,
        )
        ends = jnp.stack([picked_rows[1::2, :half], picked_rows[2::2, half:]], axis=1)
        return jnp.concatenate([picked_rows[0], ends.reshape(-1)])

    weights_in = jnp.where(
        in_parts(place_all)[None, :] == jnp.arange(places, dtype=jnp.int32)[:, None],
        in_parts(coeff)[None, :],
        0.0,
    ).astype(bf16)
    tiles_in = jnp.concatenate(parts, axis=0)
    spread = jnp.einsum(
        "akt,tpq->apkq",
        weights_in.reshape(row_blocks, col_blocks, -1),
        tiles_in,
        preferred_element_type=f32,
    ).astype(bf16)
    own_op = spread.reshape(1, orbitals, orb_rows)
    total = taylor(own_op[0], own_walkers[0], lax.axis_size("chol"))
    return (force_bias, total[None])


def solution(mesh):
    return jax.shard_map(
        body,
        mesh=mesh,
        in_specs=(
            P("wide", "chol", None),
            P("wide", None, None),
            P(),
            P(("wide", "chol"), None, None),
            P(("wide", "chol")),
            P(("wide", "chol")),
            P(("wide", "chol")),
            P(("wide", "chol")),
            P(),
            P(None, "wide"),
        ),
        out_specs=(P(None, "wide"), P("wide", "chol", None)),
        check_vma=False,
    )
```

```python
import functools

import jax
import jax.numpy as jnp
from jax import lax
from jax.experimental import pallas as pl
from jax.experimental.pallas import tpu as pltpu
from jax.sharding import PartitionSpec as P

TAYLOR = 4


SQRT_TAU = 0.1


def ring_order(size):
    half = size // 2
    return [2 * p for p in range(half)] + [2 * (size - 1 - p) + 1 for p in range(half, size)]


def series_kernel(
    pairs,
    op_ref,
    walk_ref,
    out_ref,
    op_peer,
    walk_in,
    term,
    total,
    send_buf,
    recv_buf,
    end_send,
    end_recv,
    swap_send,
    swap_recv,
    send_sem,
    recv_sem,
):
    f32 = jnp.float32
    bf16 = jnp.bfloat16
    wide = lax.axis_index("wide")
    me = lax.axis_index("chol")
    core = me % 2
    pair = me // 2
    partner = me + 1 - 2 * core
    rows = op_ref.shape[1]
    chunks = send_buf.shape[2]
    piece = send_buf.shape[3]
    peers = [((pair + j) % pairs) for j in range(1, pairs)]

    def place(chol):
        return (wide, chol)

    barrier = pltpu.get_barrier_semaphore()
    for other in [partner] + [2 * p + core for p in peers]:
        pl.semaphore_signal(
            barrier, inc=1, device_id=place(other), device_id_type=pl.DeviceIdType.MESH
        )
    pl.semaphore_wait(barrier, pairs)

    def remote(src, dst, send, recv, other):
        return pltpu.make_async_remote_copy(
            src_ref=src,
            dst_ref=dst,
            send_sem=send,
            recv_sem=recv,
            device_id=place(other),
            device_id_type=pl.DeviceIdType.MESH,
        )

    walk_swap = remote(
        walk_ref.at[1 - core], walk_in, swap_send.at[0], swap_recv.at[0], partner
    )
    op_swap = remote(op_ref, op_peer, swap_send.at[1], swap_recv.at[1], partner)
    walk_swap.start()
    op_swap.start()
    own_at = pl.ds(pl.multiple_of(core * rows, rows), rows)
    other_at = pl.ds(pl.multiple_of((1 - core) * rows, rows), rows)
    term[own_at, :] = walk_ref[core]
    total[own_at, :] = walk_ref[core].astype(f32)
    walk_swap.wait()
    term[other_at, :] = walk_in[...]
    total[other_at, :] = walk_in[...].astype(f32)
    op_swap.wait()

    def product(start, count):
        at = pl.ds(pl.multiple_of(start, piece), count)
        return jnp.dot(op_ref[at, :], term[own_at, :], preferred_element_type=f32) + jnp.dot(
            op_peer[at, :], term[other_at, :], preferred_element_type=f32
        )

    for order in range(1, TAYLOR + 1):
        copies = []
        for j, p in enumerate(peers):
            for c in range(chunks):
                slot = (order - 1, j, c)
                send_buf[slot] = product(p * (2 * rows) + c * piece, piece).astype(bf16)
                copy = remote(
                    send_buf.at[slot],
                    recv_buf.at[slot],
                    send_sem.at[slot],
                    recv_sem.at[slot],
                    2 * p + core,
                )
                copy.start()
                copies.append(copy)
        parts = [product(pair * (2 * rows) + c * piece, piece) for c in range(chunks)]
        for c in range(chunks):
            part = parts[c]
            for j in range(len(peers)):
                copies[j * chunks + c].wait()
                part = part + recv_buf[order - 1, j, c].astype(f32)
            parts[c] = (SQRT_TAU / order * part).astype(bf16)
        for c in range(chunks):
            at = pl.ds(c * piece, piece)
            term[at, :] = parts[c]
            total[at, :] += parts[c].astype(f32)
    end_send[...] = total[other_at, :].astype(bf16)
    end_swap = remote(end_send, end_recv, swap_send.at[2], swap_recv.at[2], partner)
    end_swap.start()
    out_ref[core] = total[own_at, :].astype(bf16)
    end_swap.wait()
    out_ref[1 - core] = end_recv[...]


def taylor(own_op, own_walkers, chol):
    bf16 = jnp.bfloat16
    orbitals, rows = own_op.shape
    electrons = own_walkers.shape[1]
    half = electrons // 2
    pairs = chol // 2
    chunks = 4
    piece = 2 * rows // chunks
    others = max(pairs - 1, 1)
    slots = (TAYLOR, others, chunks)
    walk = jnp.transpose(own_walkers.reshape(rows, 2, half), (1, 0, 2))
    out = pl.pallas_call(
        functools.partial(series_kernel, pairs),
        out_shape=jax.ShapeDtypeStruct((2, rows, half), bf16),
        in_specs=[pl.BlockSpec(memory_space=pltpu.VMEM)] * 2,
        out_specs=pl.BlockSpec(memory_space=pltpu.VMEM),
        scratch_shapes=[
            pltpu.VMEM((orbitals, rows), bf16),
            pltpu.VMEM((rows, half), bf16),
            pltpu.VMEM((2 * rows, half), bf16),
            pltpu.VMEM((2 * rows, half), jnp.float32),
            pltpu.VMEM(slots + (piece, half), bf16),
            pltpu.VMEM(slots + (piece, half), bf16),
            pltpu.VMEM((rows, half), bf16),
            pltpu.VMEM((rows, half), bf16),
            pltpu.SemaphoreType.DMA((3,)),
            pltpu.SemaphoreType.DMA((3,)),
            pltpu.SemaphoreType.DMA(slots),
            pltpu.SemaphoreType.DMA(slots),
        ],
        compiler_params=pltpu.CompilerParams(
            collective_id=0, has_side_effects=True, vmem_limit_bytes=32 * 1024 * 1024
        ),
    )(own_op, walk)
    return jnp.transpose(out, (1, 0, 2)).reshape(rows, electrons)


def share_kernel(
    chol,
    wide,
    bias_ref,
    noise_ref,
    hot_ref,
    place_ref,
    force_ref,
    got_ref,
    bias_in,
    got_in,
    sent,
    bias_send,
    bias_recv,
    got_send,
    got_recv,
):
    f32 = jnp.float32
    bf16 = jnp.bfloat16
    at_wide = lax.axis_index("wide")
    at_chol = lax.axis_index("chol")
    mesh_id = pl.DeviceIdType.MESH
    in_chol = [(at_wide, (at_chol + j) % chol) for j in range(1, chol)]
    in_wide = [((at_wide + j) % wide, at_chol) for j in range(1, wide)]
    barrier = pltpu.get_barrier_semaphore()
    for peer in in_chol + in_wide:
        pl.semaphore_signal(barrier, inc=1, device_id=peer, device_id_type=mesh_id)
    pl.semaphore_wait(barrier, chol + wide - 2)
    copies = []
    for j, peer in enumerate(in_chol):
        copy = pltpu.make_async_remote_copy(
            src_ref=bias_ref,
            dst_ref=bias_in.at[at_chol],
            send_sem=bias_send.at[j],
            recv_sem=bias_recv.at[j],
            device_id=peer,
            device_id_type=mesh_id,
        )
        copy.start()
        copies.append(copy)
    bias_in[at_chol] = bias_ref[...]
    for copy in copies:
        copy.wait()
    force = bias_in[0]
    for c in range(1, chol):
        force = force + bias_in[c]
    force_ref[...] = force
    field = (noise_ref[...] - SQRT_TAU * force).astype(bf16)
    coeff = jnp.dot(field, hot_ref[...], preferred_element_type=f32)
    sent[...] = jnp.concatenate([coeff, place_ref[...]], axis=0).astype(bf16)
    copies = []
    for j, peer in enumerate(in_wide):
        copy = pltpu.make_async_remote_copy(
            src_ref=sent,
            dst_ref=got_in.at[at_wide],
            send_sem=got_send.at[j],
            recv_sem=got_recv.at[j],
            device_id=peer,
            device_id_type=mesh_id,
        )
        copy.start()
        copies.append(copy)
    got_in[at_wide] = sent[...]
    for copy in copies:
        copy.wait()
    got_ref[...] = got_in[...]


def share(bias_part, aux_noise, hot, places, chol, wide):
    bf16 = jnp.bfloat16
    slots = hot.shape[1]
    rows = bias_part.shape[0] + places.shape[0]
    return pl.pallas_call(
        functools.partial(share_kernel, chol, wide),
        out_shape=(
            jax.ShapeDtypeStruct(bias_part.shape, jnp.float32),
            jax.ShapeDtypeStruct((wide, rows, slots), bf16),
        ),
        in_specs=[pl.BlockSpec(memory_space=pltpu.VMEM)] * 4,
        out_specs=(pl.BlockSpec(memory_space=pltpu.VMEM),) * 2,
        scratch_shapes=[
            pltpu.VMEM((chol,) + bias_part.shape, jnp.float32),
            pltpu.VMEM((wide, rows, slots), bf16),
            pltpu.VMEM((rows, slots), bf16),
            pltpu.SemaphoreType.DMA((chol - 1,)),
            pltpu.SemaphoreType.DMA((chol - 1,)),
            pltpu.SemaphoreType.DMA((wide - 1,)),
            pltpu.SemaphoreType.DMA((wide - 1,)),
        ],
        compiler_params=pltpu.CompilerParams(collective_id=1, has_side_effects=True),
    )(bias_part, aux_noise, hot, places)


def body(
    walkers,
    intersection_inv,
    trial_state,
    chol_tiles,
    tile_vector,
    tile_row,
    tile_col,
    tile_count,
    sources,
    aux_noise,
):
    f32 = jnp.float32
    bf16 = jnp.bfloat16
    highest = lax.Precision.HIGHEST
    walk_dev, orb_rows, electrons = walkers.shape
    slot_count, tile_size, _ = chol_tiles.shape
    orbitals = trial_state.shape[0]
    row_blocks = orbitals // tile_size
    col_blocks = orb_rows // tile_size
    walk_all, vec_dev = aux_noise.shape
    wide = lax.axis_size("wide")
    me = lax.axis_index("wide")
    live_slot = jnp.arange(slot_count, dtype=jnp.int32) < tile_count[0]
    place_own = tile_row * col_blocks + tile_col
    walker_rows = lax.all_gather(walkers, "wide", axis=0, tiled=True)
    inv_all = lax.all_gather(intersection_inv, "wide", axis=0, tiled=True)
    order = ring_order(wide)
    right = [(order[p], order[(p + 1) % wide]) for p in range(wide)]
    left = [(b, a) for a, b in right]
    spot_of = [0] * wide
    for p, idx in enumerate(order):
        spot_of[idx] = p
    turns = [0] + [turn for step in range(1, wide) for turn in (-step, step)]
    owners = jnp.asarray(
        [[order[(spot_of[idx] + turn) % wide] for turn in turns] for idx in range(wide)], jnp.int32
    )[me]
    picker = (sources[:, None] == jnp.arange(walk_all, dtype=jnp.int32)[None, :]).astype(bf16)
    picked = jnp.einsum("jw,wmn->jmn", picker, walker_rows, preferred_element_type=f32).astype(bf16)
    picked_inv = jnp.einsum("jw,wnk->jnk", picker, inv_all, preferred_element_type=f32).astype(bf16)
    theta_new = jnp.einsum("jmn,jnk->jmk", picked, picked_inv, preferred_element_type=f32).astype(
        bf16
    )
    own_walkers = lax.dynamic_slice_in_dim(picked, me * walk_dev, walk_dev, 0)
    row_hot = (tile_row[:, None] == jnp.arange(row_blocks, dtype=jnp.int32)[None, :]).astype(f32)
    col_hot = (tile_col[:, None] == jnp.arange(col_blocks, dtype=jnp.int32)[None, :]).astype(f32)
    live = live_slot.astype(f32)
    vec_hot = (tile_vector[:, None] == jnp.arange(vec_dev, dtype=jnp.int32)[None, :]).astype(f32)
    trial_blocks = trial_state.reshape(row_blocks, tile_size * electrons)
    tile_rows = jnp.dot(row_hot.astype(bf16), trial_blocks, preferred_element_type=f32).astype(bf16)
    tile_rows = tile_rows.reshape(slot_count, tile_size, electrons)
    projected = jnp.einsum(
        "tpq,tpn->tqn", chol_tiles, tile_rows, preferred_element_type=f32
    ).astype(bf16)
    theta_blocks = theta_new.reshape(walk_all, col_blocks, tile_size, electrons)
    scores = jnp.einsum("tqn,wcqn->wtc", projected, theta_blocks, preferred_element_type=f32)
    scores = jnp.sum(scores * col_hot[None], axis=2) * live[None, :]
    bias_part = jnp.dot(scores, vec_hot, precision=highest)
    half = slot_count // 2
    going, coming = chol_tiles[:half], chol_tiles[half:]
    parts = [chol_tiles]
    for step in range(1, wide):
        going = lax.ppermute(going, "wide", right)
        coming = lax.ppermute(coming, "wide", left)
        parts += [going, coming]
    force_bias, got = share(
        bias_part,
        aux_noise,
        (vec_hot * live[:, None]).T.astype(bf16),
        jnp.broadcast_to(place_own.astype(f32)[None], (8, slot_count)),
        lax.axis_size("chol"),
        wide,
    )
    got = got.astype(f32)
    coeff = lax.dynamic_index_in_dim(got, me * walk_dev, 1, keepdims=False)
    place_all = got[:, walk_all].astype(jnp.int32)
    places = row_blocks * col_blocks

    def in_parts(whole):
        picked_rows = jnp.sum(
            jnp.where(
                owners[:, None, None] == jnp.arange(wide, dtype=jnp.int32)[None, :, None],
                whole[None],
                jnp.zeros((), whole.dtype),
            ),
            axis=1,
        )
        ends = jnp.stack([picked_rows[1::2, :half], picked_rows[2::2, half:]], axis=1)
        return jnp.concatenate([picked_rows[0], ends.reshape(-1)])

    weights_in = jnp.where(
        in_parts(place_all)[None, :] == jnp.arange(places, dtype=jnp.int32)[:, None],
        in_parts(coeff)[None, :],
        0.0,
    ).astype(bf16)
    tiles_in = jnp.concatenate(parts, axis=0)
    spread = jnp.einsum(
        "akt,tpq->apkq",
        weights_in.reshape(row_blocks, col_blocks, -1),
        tiles_in,
        preferred_element_type=f32,
    ).astype(bf16)
    own_op = spread.reshape(1, orbitals, orb_rows)
    total = taylor(own_op[0], own_walkers[0], lax.axis_size("chol"))
    return (force_bias, total[None])


def solution(mesh):
    return jax.shard_map(
        body,
        mesh=mesh,
        in_specs=(
            P("wide", "chol", None),
            P("wide", None, None),
            P(),
            P(("wide", "chol"), None, None),
            P(("wide", "chol")),
            P(("wide", "chol")),
            P(("wide", "chol")),
            P(("wide", "chol")),
            P(),
            P(None, "wide"),
        ),
        out_specs=(P(None, "wide"), P("wide", "chol", None)),
        check_vma=False,
    )
```
